128 devices in a mesh: row: 8 (over z, core), col: 16 (over x, y).
Axes of the slice: x: 4, y: 4, z: 4, core: 2. Of those that a mesh axis runs over, the one named last changes fastest.
Arguments:
- root_front: float32 [12288, 12288], P('row', 'col'), may hold values from -9 to 9, as said below
- child_updates: float32 [12288, 6144], P('row', 'col'), may hold values from -9 to 9, as said below
- row_targets: int32 [2, 48], replicated, may hold values from 0 to 95, as said below
- column_targets: int32 [2, 48], replicated, may hold values from 0 to 95, as said below
- pivot_inverse: float32 [2, 512, 512], replicated, may hold values from -0.1 to 0.1, as said below
Outputs:
- panel_factors: float32 [12288, 1024], P('row')
- schur_front: float32 [12288, 12288], P('row', 'col')
The draws below stay inside these ranges and needn't reach their ends.
Inputs may be any that keep to these rules, and one draw needn't show every extreme that they name: `row_targets`: each row is increasing and holds exactly half of every aligned group of 8 consecutive global tiles. The 12 tiles of a child held by one row device fall in exactly half of the classes modulo 8, 3 in each. `column_targets`: row c holds the tiles of row c of row_targets, ordered by class modulo 16 and increasing within a class; each class holds 3 tiles, so those on column device q are of class q. `root_front`: in global tile order on rows and columns the front is symmetric. `child_updates`: each child, with its column tiles put back in the order of its row list, is symmetric. `pivot_inverse`: both matrices are lower triangular.
All inputs are finite; a program needn't handle non-finite values.
Results may differ from the reference program's by a relative error of at most 0.0001.
Values sent between devices are 32-bit elements; how exact they have to be, the bound alone decides.
No kernel may reach another device: no remote copies, remote signals or barrier semaphores. Data moves between devices by JAX's collectives and lax.ppermute only.
A program may use at most 128 MiB of HBM per device.

```python
import math
import jax
import jax.numpy as jnp
from jax import lax

ROOT = 12288
CHILD = 6144
TILE = 128
PANEL = 512
N_ROW = 8
N_COL = 16


def tile_maps(key):
    base = jax.random.fold_in(key, 101)
    tiles_side = ROOT // TILE
    groups = tiles_side // N_ROW
    capacity = 2 * groups // N_ROW
    halves = N_ROW // 2
    group_ids = jnp.arange(groups, dtype=jnp.int32)
    residues = jnp.arange(N_ROW, dtype=jnp.int32)
    block_ids = group_ids // capacity
    row_lists = []
    column_lists = []
    positions = []
    for child in range(2):
        child_key = jax.random.fold_in(base, child)
        shuffled = jax.random.permutation(jax.random.fold_in(child_key, 10), N_ROW)
        inside = (jnp.argsort(shuffled) < halves).astype(jnp.int32)
        offset = jax.random.randint(jax.random.fold_in(child_key, 20), (), 0, 4)
        if halves == 4:
            flips = (block_ids + offset) // 2 % 2
        else:
            flips = (block_ids + offset) % 2
        chosen = (inside[None, :] + flips[:, None]) % 2
        scores = (1 - chosen) * N_ROW + residues[None, :]
        ranked = jnp.argsort(scores, axis=1)[:, :halves].astype(jnp.int32)
        tiles = (group_ids[:, None] * N_ROW + ranked).reshape(-1).astype(jnp.int32)
        column_order = jnp.argsort(tiles % N_COL * tiles_side + tiles).astype(jnp.int32)
        row_lists.append(tiles)
        column_lists.append(tiles[column_order])
        positions.append(column_order)
    return (jnp.stack(row_lists), jnp.stack(column_lists), jnp.stack(positions))


def noise_field(key, side):
    values = jnp.clip(jax.random.normal(key, (side, side), jnp.float32), -6.0, 6.0)
    return (values + values.T) * math.sqrt(0.5)


def draw_row_targets(key, part):
    return tile_maps(key)[0]


def draw_column_targets(key, part):
    return tile_maps(key)[1]


def draw_root_front(key, part):
    tiles_side = ROOT // TILE
    row_local = tiles_side // N_ROW
    col_local = tiles_side // N_COL
    stored = jnp.arange(tiles_side, dtype=jnp.int32)
    row_global = stored % row_local * N_ROW + stored // row_local
    column_global = stored % col_local * N_COL + stored // col_local
    symmetric = noise_field(jax.random.fold_in(key, 300), ROOT)
    tiled = symmetric.reshape(tiles_side, TILE, tiles_side, TILE)
    tiled = tiled[row_global][:, :, column_global, :]
    return tiled.reshape(ROOT, ROOT)


def draw_child_updates(key, part):
    child_side = CHILD // TILE
    positions = tile_maps(key)[2]
    blocks = []
    for child in range(2):
        symmetric = noise_field(jax.random.fold_in(key, 400 + child), CHILD)
        tiled = symmetric.reshape(child_side, TILE, child_side, TILE)[:, :, positions[child], :]
        blocks.append(tiled.reshape(CHILD, CHILD))
    return jnp.concatenate(blocks, axis=0)


def draw_pivot_inverse(key, part):
    mats = []
    for step in range(2):
        step_key = jax.random.fold_in(key, 500 + step)
        lower = jnp.clip(jax.random.normal(jax.random.fold_in(step_key, 1), (PANEL, PANEL), jnp.float32), -2.2, 2.2)
        lower = jnp.tril(lower, -1) * (0.25 / math.sqrt(PANEL))
        diagonal = jax.random.uniform(jax.random.fold_in(step_key, 2), (PANEL,), jnp.float32, 0.01, 0.03)
        mats.append(lower + jnp.diag(diagonal))
    return jnp.stack(mats)


def setup_inputs(seed: int = 0) -> dict:
    key_list = jax.random.split(jax.random.key(seed), 6)
    root_front = draw_root_front(jax.random.fold_in(key_list[5], 71), 0)
    child_updates = draw_child_updates(jax.random.fold_in(key_list[5], 71), 0)
    row_targets = draw_row_targets(jax.random.fold_in(key_list[5], 71), 0)
    column_targets = draw_column_targets(jax.random.fold_in(key_list[5], 71), 0)
    pivot_inverse = draw_pivot_inverse(jax.random.fold_in(key_list[5], 71), 0)
    return {"root_front": root_front, "child_updates": child_updates, "row_targets": row_targets, "column_targets": column_targets, "pivot_inverse": pivot_inverse}


def reference(root_front, child_updates, row_targets, column_targets, pivot_inverse):
    tiles_side = ROOT // TILE
    row_local = tiles_side // N_ROW
    col_local = tiles_side // N_COL
    child_side = CHILD // TILE
    panel_tiles = PANEL // TILE

    def row_storage(global_tile):
        return ((global_tile % N_ROW) * row_local + global_tile // N_ROW).astype(jnp.int32)

    def column_storage(global_tile):
        return ((global_tile % N_COL) * col_local + global_tile // N_COL).astype(jnp.int32)

    stored = jnp.arange(tiles_side, dtype=jnp.int32)
    row_global = (stored % row_local) * N_ROW + stored // row_local
    column_global = (stored % col_local) * N_COL + stored // col_local
    tiled = root_front.reshape(tiles_side, TILE, tiles_side, TILE)
    for child in range(2):
        block = child_updates[child * CHILD:(child + 1) * CHILD]
        block = block.reshape(child_side, TILE, child_side, TILE).transpose(0, 2, 1, 3)
        rows_at = row_storage(row_targets[child])
        columns_at = column_storage(column_targets[child])
        tiled = tiled.at[rows_at[:, None], :, columns_at[None, :], :].add(block)
    current = tiled.reshape(ROOT, ROOT)
    transpose_rows = row_storage(column_global)
    factors = []
    for step in range(2):
        panel_columns = column_storage(jnp.arange(panel_tiles, dtype=jnp.int32) + step * panel_tiles)
        panel = current.reshape(ROOT, tiles_side, TILE)[:, panel_columns, :].reshape(ROOT, PANEL)
        factor = jnp.dot(panel, pivot_inverse[step].T, precision=lax.Precision.HIGHEST,
                         preferred_element_type=jnp.float32)
        keep = jnp.repeat(row_global >= (step + 1) * panel_tiles, TILE)[:, None]
        factor = jnp.where(keep, factor, 0.0)
        column_rows = factor.reshape(tiles_side, TILE, PANEL)[transpose_rows].reshape(ROOT, PANEL)
        current = current - lax.dot_general(factor, column_rows, (((1,), (1,)), ((), ())),
                                            precision=lax.Precision.HIGHEST,
                                            preferred_element_type=jnp.float32)
        factors.append(factor)
    return jnp.concatenate(factors, axis=1), current
```

```python
import functools

import jax
import jax.numpy as jnp
from jax import lax
from jax.experimental import pallas as pl
from jax.experimental.pallas import tpu as pltpu
from jax.sharding import PartitionSpec as P

TILE = 128
PANEL = 512
BLOCK = 384
SHIFTS = ((0, 0), (0, 1), (1, 0), (1, 1), (3, 0), (3, 1), (2, 0), (2, 1))
NEAR = (0, -1, 1, 2)
ANY = pl.BlockSpec(memory_space=pl.ANY)
SMEM = pl.BlockSpec(memory_space=pltpu.SMEM)
VMEM = pl.BlockSpec(memory_space=pltpu.VMEM)
NT = (((1,), (1,)), ((), ()))
NN = (((1,), (0,)), ((), ()))


def move_row(x, dz, dc):
    pairs = [(2 * z + c, 2 * ((z + dz) % 4) + (c + dc) % 2) for z in range(4) for c in range(2)]
    return lax.ppermute(x, "row", pairs)


def swap_chips(x, other):
    return lax.ppermute(x, "row", [(2 * z + c, 2 * other[z] + c) for z in range(4) for c in range(2)])


def move_col(x, dx, dy):
    pairs = [(4 * a + b, 4 * ((a + dx) % 4) + (b + dy) % 4) for a in range(4) for b in range(4)]
    return lax.ppermute(x, "col", pairs)


def swap_halves(x):
    other = (3, 2, 1, 0)
    return lax.ppermute(x, "col", [(4 * a + b, 4 * other[a] + b) for a in range(4) for b in range(4)])


def split(x):
    high = x.astype(jnp.bfloat16)
    return high, (x - high.astype(jnp.float32)).astype(jnp.bfloat16)


def dot3(a, b, dims):
    d = functools.partial(lax.dot_general, dimension_numbers=dims, preferred_element_type=jnp.float32)
    return d(a[0], b[0]) + (d(a[0], b[1]) + d(a[1], b[0]))


def shifted(r, dz, dc):
    return 2 * lax.rem(r // 2 + dz + 4, 4) + lax.rem(r % 2 + dc, 2)


def child_class(targets, source, p):
    return targets[source // 4, 12 * (source % 4) + p] % 8


def holds(targets, source, r):
    hit = child_class(targets, source, 0) == r
    for p in range(1, 4):
        hit = hit | (child_class(targets, source, p) == r)
    return hit


def pack_kernel(first, last, targets, child, *outs):
    r = lax.axis_index("row")
    for i, (dz, dc) in enumerate(SHIFTS):
        dest = shifted(r, dz, dc)
        p = jnp.int32(0)
        for n in range(1, 4):
            p = jnp.where(child_class(targets, r, n) == dest, n, p)
        for j in range(3):
            rows = pl.ds(pl.multiple_of(TILE * (4 * j + p), TILE), TILE)
            outs[i][TILE * j : TILE * (j + 1), :] = child[rows, first:last]


def pack(row_targets, child, first, last):
    return pl.pallas_call(
        functools.partial(pack_kernel, first, last),
        grid=(1,),
        out_shape=[jax.ShapeDtypeStruct((BLOCK, last - first), jnp.float32)] * 8,
        in_specs=[SMEM, pl.BlockSpec((4 * BLOCK, last), lambda i: (0, 0))],
        out_specs=[VMEM] * 8,
        name=f"pack_{first}",
    )(row_targets, child)


def panel_kernel(row_targets, column_targets, root, *rest):
    messages, near, far, total = rest[:8], rest[8], rest[9], rest[10]
    r, q = lax.axis_index("row"), lax.axis_index("col")
    total[...] = root[...]
    for i, (dz, dc) in enumerate(SHIFTS):
        source = shifted(r, -dz, dc)
        first = column_targets[source // 4, 3 * q] // 16 == 0

        @pl.when(holds(row_targets, source, r) & first)
        def _(i=i, source=source):
            rows = pl.ds(pl.multiple_of(BLOCK * (source % 4), BLOCK), BLOCK)
            total[rows, :] += messages[i][...]

    near[...] = total[: 2 * BLOCK, :]
    far[...] = total[2 * BLOCK :, :]


def panel_of(row_targets, column_targets, root, messages):
    return pl.pallas_call(
        panel_kernel,
        grid=(1,),
        out_shape=[jax.ShapeDtypeStruct((2 * BLOCK, TILE), jnp.float32)] * 2,
        in_specs=[SMEM, SMEM, pl.BlockSpec((4 * BLOCK, TILE), lambda i: (0, 0))] + [VMEM] * 8,
        out_specs=[VMEM] * 2,
        scratch_shapes=[pltpu.VMEM((4 * BLOCK, TILE), jnp.float32)],
        name="panel",
    )(row_targets, column_targets, root, *messages)


def rows_kernel(row_targets, column_targets, *rest):
    tops, firsts, out, corner, total = rest[:8], rest[8:12], rest[12], rest[13], rest[14]
    r, q = lax.axis_index("row"), lax.axis_index("col")
    for piece, (dz, dc) in zip(tops, SHIFTS, strict=True):
        rows = pl.ds(pl.multiple_of(TILE * shifted(r, -dz, dc), TILE), TILE)
        for m in range(6):
            total[m, rows, :] = piece[:, TILE * m : TILE * (m + 1)]
    half = r // 4
    core = r % 2
    where_from = ((half, core), (1 - half, core), (half, 1 - core), (1 - half, 1 - core))
    for piece, (child, part) in zip(firsts, where_from, strict=True):
        for n in range(2):
            tile = row_targets[child, 2 * part + n]
            rows = pl.ds(pl.multiple_of(TILE * tile, TILE), TILE)
            for m in range(3):
                column = column_targets[child, 3 * q + m] // 16
                total[column, rows, :] += piece[TILE * n : TILE * (n + 1), TILE * m : TILE * (m + 1)]
    for m in range(6):
        out[:, TILE * m : TILE * (m + 1)] = total[m]
    corner[...] = total[0, pl.ds(pl.multiple_of(PANEL + 2 * TILE * core, TILE), 2 * TILE), :]


def rows_of(row_targets, column_targets, tops, firsts):
    return pl.pallas_call(
        rows_kernel,
        out_shape=[
            jax.ShapeDtypeStruct((2 * PANEL, 6 * TILE), jnp.float32),
            jax.ShapeDtypeStruct((2 * TILE, TILE), jnp.float32),
        ],
        in_specs=[SMEM, SMEM] + [VMEM] * 12,
        out_specs=[VMEM] * 2,
        scratch_shapes=[pltpu.VMEM((6, 2 * PANEL, TILE), jnp.float32)],
        name="rows",
    )(row_targets, column_targets, *tops, *firsts)


def columns_kernel(inverse, rows, *rest):
    pieces = rest[:8]
    c_high, c_low, g_high, g_low, l_high, l_low, corner = rest[8:]
    r, q = lax.axis_index("row"), lax.axis_index("col")
    core = r % 2
    for n, piece in enumerate(pieces):
        part = core if n < 4 else 1 - core
        tile = lax.rem(q % 4 + NEAR[n % 4] + 4, 4)
        corner[tile, pl.ds(pl.multiple_of(2 * TILE * part, TILE), 2 * TILE), :] = piece[...]
    l_high[...], l_low[...] = split(inverse[...])
    l0 = (l_high[0], l_low[0])
    l1 = (l_high[1], l_low[1])
    block = jnp.concatenate([corner[t] for t in range(4)], axis=1)
    g = split(dot3(split(block), l0, NT))
    g_high[...], g_low[...] = g
    at = lax.broadcasted_iota(jnp.int32, (PANEL, 6 * TILE), 1)
    c0 = dot3(l0, split(rows[:PANEL]), NN)
    c0_halves = split(jnp.where((at >= TILE) | (q >= 4), c0, 0.0))
    c_high[:PANEL], c_low[:PANEL] = c0_halves
    later = rows[PANEL:] - dot3(g, c0_halves, NN)
    c1 = dot3(l1, split(later), NN)
    c_high[PANEL:], c_low[PANEL:] = split(jnp.where((at >= TILE) | (q >= 8), c1, 0.0))


def columns_of(inverse, rows, pieces):
    bf16 = jnp.bfloat16
    return pl.pallas_call(
        columns_kernel,
        out_shape=[jax.ShapeDtypeStruct((2 * PANEL, 6 * TILE), bf16)] * 2
        + [jax.ShapeDtypeStruct((PANEL, PANEL), bf16)] * 2
        + [jax.ShapeDtypeStruct((2, PANEL, PANEL), bf16)] * 2,
        in_specs=[VMEM] * 10,
        out_specs=[VMEM] * 6,
        scratch_shapes=[pltpu.VMEM((4, PANEL, TILE), jnp.float32)],
        name="columns",
    )(inverse, rows, *pieces)


def front_kernel(row_targets, column_targets, *rest):
    c_high, c_low, g_high, g_low, l_high, l_low, root = rest[:7]
    pieces = (rest[7:12], rest[12:17])
    first, others = rest[17:25], rest[25:33]
    factors, front, panel, child, panel_sems, child_sems = rest[33:]
    r, q = lax.axis_index("row"), lax.axis_index("col")
    x, y = q // 4, q % 4
    k = pl.program_id(0)

    def child_copies(i, source):
        return (
            pltpu.make_async_copy(first[i], child.at[source, :, :TILE], child_sems.at[source, 0]),
            pltpu.make_async_copy(others[i], child.at[source, :, TILE:], child_sems.at[source, 1]),
        )

    @pl.when(k == 0)
    def _():
        for part in range(2):
            for v in range(5):
                source_ref = pieces[part][v]
                for u in range(4):
                    outer, inner = NEAR[min(v, 3)], NEAR[u]
                    dx, dy = (inner, outer) if part == 0 else (outer, inner)
                    px, py = lax.rem(x + dx + 4, 4), lax.rem(y + dy + 4, 4)
                    half = px // 2
                    tile = jnp.where((px == 0) | (px == 3), 0, 4) + py
                    start = BLOCK * (2 * half + part) + (BLOCK // 2 if v == 4 else 0)
                    count = BLOCK if v < 3 else BLOCK // 2
                    pltpu.make_async_copy(
                        source_ref.at[u],
                        panel.at[tile, pl.ds(pl.multiple_of(start, BLOCK // 2), count), :],
                        panel_sems.at[2 * half + part],
                    ).start()
        for i, (dz, dc) in enumerate(SHIFTS):
            source = shifted(r, -dz, dc)

            @pl.when(holds(row_targets, source, r))
            def _(i=i, source=source):
                for c in child_copies(i, source):
                    c.start()

    here = pl.ds(pl.multiple_of(BLOCK * k, BLOCK), BLOCK)
    arrived = panel.at[:, here, :]
    pltpu.make_async_copy(arrived, arrived, panel_sems.at[k]).wait()
    p0 = jnp.concatenate([panel[t, here, :] for t in range(4)], axis=1)
    p1 = jnp.concatenate([panel[t, here, :] for t in range(4, 8)], axis=1)
    at = lax.broadcasted_iota(jnp.int32, (BLOCK, PANEL), 0)
    later = (at >= TILE) | (k > 0)
    f0 = dot3(split(p0), (l_high[0], l_low[0]), NT)
    f0 = jnp.where(later | (r >= 4), f0, 0.0)
    factors[:, :PANEL] = f0
    f0 = split(f0)
    p1 = p1 - dot3(f0, (g_high[...], g_low[...]), NT)
    f1 = dot3(split(p1), (l_high[1], l_low[1]), NT)
    f1 = jnp.where(later, f1, 0.0)
    factors[:, PANEL:] = f1
    f1 = split(f1)
    both = (jnp.concatenate([f0[0], f1[0]], axis=1), jnp.concatenate([f0[1], f1[1]], axis=1))
    front[...] = root[...] - dot3(both, (c_high[...], c_low[...]), NN)
    for c in range(2):
        source = 4 * c + k

        @pl.when(holds(row_targets, source, r))
        def _(c=c, source=source):
            for copy in child_copies(0, source):
                copy.wait()
            for m in range(3):
                column = column_targets[c, 3 * q + m] // 16
                columns = pl.ds(pl.multiple_of(TILE * column, TILE), TILE)
                front[:, columns] += child[source, :, TILE * m : TILE * (m + 1)]


def front_of(row_targets, column_targets, columns, root, pieces, first, others):
    def whole(a):
        return pl.BlockSpec(a.shape, lambda k: (0,) * a.ndim, pipeline_mode=pl.Buffered(1))

    return pl.pallas_call(
        front_kernel,
        grid=(4,),
        out_shape=[
            jax.ShapeDtypeStruct((4 * BLOCK, 2 * PANEL), jnp.float32),
            jax.ShapeDtypeStruct((4 * BLOCK, 6 * TILE), jnp.float32),
        ],
        in_specs=[SMEM, SMEM]
        + [whole(a) for a in columns]
        + [pl.BlockSpec((BLOCK, 6 * TILE), lambda k: (k, 0))]
        + [ANY] * 26,
        out_specs=[
            pl.BlockSpec((BLOCK, 2 * PANEL), lambda k: (k, 0)),
            pl.BlockSpec((BLOCK, 6 * TILE), lambda k: (k, 0)),
        ],
        scratch_shapes=[
            pltpu.VMEM((8, 4 * BLOCK, TILE), jnp.float32),
            pltpu.VMEM((8, BLOCK, 3 * TILE), jnp.float32),
            pltpu.SemaphoreType.DMA((4,)),
            pltpu.SemaphoreType.DMA((8, 2)),
        ],
        name="front",
    )(row_targets, column_targets, *columns, root, *pieces[0], *pieces[1], *first, *others)


def relay(x, move):
    before, after = move(x, 1), move(x, -1)
    n = x.shape[-2] // 2
    low = move(before[..., :n, :], 1)
    high = move(after[..., n:, :], -1)
    return x, before, after, low, high


def stacked(parts):
    own, before, after, low, high = parts
    return jnp.stack([own, before, after, jnp.concatenate([low, high], axis=-2)])


def on_device(root_front, child_updates, row_targets, column_targets, pivot_inverse):
    r, q = lax.axis_index("row"), lax.axis_index("col")
    z, core, x = r // 2, r % 2, q // 4

    messages = pack(row_targets, child_updates, 0, TILE)
    first = [messages[0]] + [move_row(m, *s) for m, s in zip(messages[1:], SHIFTS[1:], strict=True)]

    top = root_front[:TILE]
    tops = [top] + [None] * 7
    for i in (2, 4, 6):
        tops[i] = move_row(top, *SHIFTS[i])
    for i in (0, 2, 4, 6):
        tops[i + 1] = move_row(tops[i], 0, 1)
    upper = child_updates[2 * TILE : 4 * TILE]
    mine = jnp.where(core == 0, child_updates[: 2 * TILE], move_row(upper, 0, 1))
    mine = jnp.where(z % 2 == 0, mine, swap_chips(mine, (1, 0, 3, 2)))
    theirs = swap_chips(mine, (3, 2, 1, 0))
    firsts = [mine, theirs, move_row(mine, 0, 1), move_row(theirs, 0, 1)]
    rows, corner = rows_of(row_targets, column_targets, tops, firsts)

    messages = pack(row_targets, child_updates, TILE, 3 * TILE)
    others = [messages[0]] + [move_row(m, *s) for m, s in zip(messages[1:], SHIFTS[1:], strict=True)]

    near, far = panel_of(row_targets, column_targets, root_front, first)
    piece = jnp.where(x < 2, near, swap_halves(far))
    along_x = lambda v, d: move_col(v, d, 0)
    along_y = lambda v, d: move_col(v, 0, d)
    a = relay(stacked(relay(piece[:BLOCK], along_x)), along_y)
    b = relay(stacked(relay(piece[BLOCK:], along_y)), along_x)

    spread = [move_col(corner, d, 0) for d in (1, 2, -1)]
    corner = jnp.where(x == 0, corner, jnp.where(x == 1, spread[0], jnp.where(x == 2, spread[1], spread[2])))
    corners = [corner] + [move_col(corner, 0, -d) for d in NEAR[1:]]
    corners = corners + [move_row(c, 0, 1) for c in corners]
    columns = columns_of(pivot_inverse, rows, corners)

    factors, front = front_of(row_targets, column_targets, columns, root_front, (a, b), first, others)
    return factors, front


def solution(mesh):
    return jax.shard_map(
        on_device,
        mesh=mesh,
        in_specs=(P("row", "col"), P("row", "col"), P(), P(), P()),
        out_specs=(P("row", None), P("row", "col")),
        check_vma=False,
    )
```

```python
import functools

import jax
import jax.numpy as jnp
from jax import lax
from jax.experimental import pallas as pl
from jax.experimental.pallas import tpu as pltpu
from jax.sharding import PartitionSpec as P

TILE = 128
PANEL = 512
PER = 1
BLOCK = 384
SHIFTS = ((0, 0), (0, 1), (1, 0), (1, 1), (3, 0), (3, 1), (2, 0), (2, 1))
NEAR = (0, -1, 1, 2)
ANY = pl.BlockSpec(memory_space=pl.ANY)
SMEM = pl.BlockSpec(memory_space=pltpu.SMEM)
VMEM = pl.BlockSpec(memory_space=pltpu.VMEM)
NN = (((1,), (0,)), ((), ()))


def move_row(x, dz, dc):
    pairs = [(2 * z + c, 2 * ((z + dz) % 4) + (c + dc) % 2) for z in range(4) for c in range(2)]
    return lax.ppermute(x, "row", pairs)


def swap_chips(x, other):
    return lax.ppermute(x, "row", [(2 * z + c, 2 * other[z] + c) for z in range(4) for c in range(2)])


def move_col(x, dx, dy):
    pairs = [(4 * a + b, 4 * ((a + dx) % 4) + (b + dy) % 4) for a in range(4) for b in range(4)]
    return lax.ppermute(x, "col", pairs)


def swap_halves(x):
    other = (3, 2, 1, 0)
    return lax.ppermute(x, "col", [(4 * a + b, 4 * other[a] + b) for a in range(4) for b in range(4)])


def split(x):
    high = x.astype(jnp.bfloat16)
    return high, (x - high.astype(jnp.float32)).astype(jnp.bfloat16)


def dot3(a, b):
    d = functools.partial(lax.dot_general, dimension_numbers=NN, preferred_element_type=jnp.float32)
    return d(a[0], b[0]) + (d(a[0], b[1]) + d(a[1], b[0]))


def below(l, b):
    n = PANEL // 2
    top = dot3(tuple(h[:n, :n] for h in l), tuple(h[:n] for h in b))
    return jnp.concatenate([top, dot3(tuple(h[n:] for h in l), b)], axis=0)


def above(a, u):
    n = PANEL // 2
    left = dot3(tuple(h[:, :n] for h in a), tuple(h[:n, :n] for h in u))
    return jnp.concatenate([left, dot3(a, tuple(h[:, n:] for h in u))], axis=1)


def shifted(r, dz, dc):
    return 2 * lax.rem(r // 2 + dz + 4, 4) + lax.rem(r % 2 + dc, 2)


def child_class(targets, source, p):
    return targets[source // 4, 12 * (source % 4) + p] % 8


def holds(targets, source, r):
    hit = child_class(targets, source, 0) == r
    for p in range(1, 4):
        hit = hit | (child_class(targets, source, p) == r)
    return hit


def pack_kernel(first, last, targets, child, *outs):
    r = lax.axis_index("row")
    for i, (dz, dc) in enumerate(SHIFTS):
        dest = shifted(r, dz, dc)
        p = jnp.int32(0)
        for n in range(1, 4):
            p = jnp.where(child_class(targets, r, n) == dest, n, p)
        for j in range(3):
            rows = pl.ds(pl.multiple_of(TILE * (4 * j + p), TILE), TILE)
            outs[i][TILE * j : TILE * (j + 1), :] = child[rows, first:last]


def pack(row_targets, child, first, last):
    return pl.pallas_call(
        functools.partial(pack_kernel, first, last),
        grid=(1,),
        out_shape=[jax.ShapeDtypeStruct((BLOCK, last - first), jnp.float32)] * 8,
        in_specs=[SMEM, pl.BlockSpec((4 * BLOCK, last), lambda i: (0, 0))],
        out_specs=[VMEM] * 8,
    )(row_targets, child)


def pack_all_kernel(targets, child, out):
    r = lax.axis_index("row")
    for dest in range(8):
        p = jnp.int32(0)
        for n in range(1, 4):
            p = jnp.where(child_class(targets, r, n) == dest, n, p)
        for j in range(3):
            rows = pl.ds(pl.multiple_of(TILE * (4 * j + p), TILE), TILE)
            out[dest, TILE * j : TILE * (j + 1), :] = child[rows, TILE:]


def pack_all(row_targets, child):
    return pl.pallas_call(
        pack_all_kernel,
        grid=(1,),
        out_shape=jax.ShapeDtypeStruct((8, BLOCK, 2 * TILE), jnp.float32),
        in_specs=[SMEM, pl.BlockSpec((4 * BLOCK, 3 * TILE), lambda i: (0, 0))],
        out_specs=VMEM,
        name="pack_all",
    )(row_targets, child)


def inverse_kernel(inverse, l_high, l_low, u_high, u_low):
    for step in range(2):
        l_high[step], l_low[step] = split(inverse[step])
        u_high[step], u_low[step] = split(inverse[step].T)


def inverse_of(inverse):
    return pl.pallas_call(
        inverse_kernel,
        out_shape=[jax.ShapeDtypeStruct((2, PANEL, PANEL), jnp.bfloat16)] * 4,
        in_specs=[VMEM],
        out_specs=[VMEM] * 4,
        name="inverse",
    )(inverse)


def panel_kernel(row_targets, column_targets, root, *rest):
    messages, near, far, tile, total = rest[:8], rest[8], rest[9], rest[10], rest[11]
    r, q = lax.axis_index("row"), lax.axis_index("col")
    total[...] = root[...]
    for i, (dz, dc) in enumerate(SHIFTS):
        source = shifted(r, -dz, dc)
        first = column_targets[source // 4, 3 * q] // 16 == 0

        @pl.when(holds(row_targets, source, r) & first)
        def _(i=i, source=source):
            rows = pl.ds(pl.multiple_of(BLOCK * (source % 4), BLOCK), BLOCK)
            total[rows, :] += messages[i][...]

    near[...] = total[: 2 * BLOCK, :]
    far[...] = total[2 * BLOCK :, :]
    tile[...] = total[:TILE, :]


def panel_of(row_targets, column_targets, root, messages):
    return pl.pallas_call(
        panel_kernel,
        grid=(1,),
        out_shape=[jax.ShapeDtypeStruct((2 * BLOCK, TILE), jnp.float32)] * 2
        + [jax.ShapeDtypeStruct((TILE, TILE), jnp.float32)],
        in_specs=[SMEM, SMEM, pl.BlockSpec((4 * BLOCK, TILE), lambda i: (0, 0))] + [VMEM] * 8,
        out_specs=[VMEM] * 3,
        scratch_shapes=[pltpu.VMEM((4 * BLOCK, TILE), jnp.float32)],
        name="panel",
    )(row_targets, column_targets, root, *messages)


def first_sources(r):
    half, core = r // 4, r % 2
    return (half, core), (1 - half, core), (half, 1 - core), (1 - half, 1 - core)


def columns_kernel(row_targets, column_targets, l_high, l_low, u_high, u_low, *rest):
    tops, firsts, pieces = rest[:8], rest[8:12], rest[12:20]
    c_high, c_low, g_high, g_low, corner, rows = rest[20:]
    r, q = lax.axis_index("row"), lax.axis_index("col")
    for piece, (dz, dc) in zip(tops, SHIFTS, strict=True):
        here = pl.ds(pl.multiple_of(TILE * shifted(r, -dz, dc), TILE), TILE)
        for m in range(6):
            rows[m, here, :] = piece[:, TILE * m : TILE * (m + 1)]
    for piece, (child, part) in zip(firsts, first_sources(r), strict=True):
        for n in range(2):
            here = pl.ds(pl.multiple_of(TILE * row_targets[child, 2 * part + n], TILE), TILE)
            for m in range(3):
                column = column_targets[child, 3 * q + m] // 16
                rows[column, here, :] += piece[TILE * n : TILE * (n + 1), TILE * m : TILE * (m + 1)]
    core = r % 2
    for n, piece in enumerate(pieces):
        part = core if n < 4 else 1 - core
        tile = lax.rem(q % 4 + NEAR[n % 4] + 4, 4)
        chip = jnp.where(r // 2 >= 2, r // 2, 3 - r // 2)
        for m in range(2):
            below_first = 2 * (chip if m == 0 else 5 - chip) + part - 4
            corner[tile, pl.ds(pl.multiple_of(TILE * below_first, TILE), TILE), :] = piece[m]
    block = jnp.concatenate([corner[t] for t in range(4)], axis=1)
    g = above(split(block), (u_high[0], u_low[0]))
    g_high[...], g_low[...] = split(g.T)
    at = lax.broadcasted_iota(jnp.int32, (PANEL, 6 * TILE), 1)
    r0 = jnp.concatenate([rows[m, :PANEL] for m in range(6)], axis=1)
    c0 = below((l_high[0], l_low[0]), split(r0))
    c0 = split(jnp.where((at >= TILE) | (q >= 4), c0, 0.0))
    c_high[:PANEL], c_low[:PANEL] = c0
    r1 = jnp.concatenate([rows[m, PANEL:] for m in range(6)], axis=1)
    r1 = r1 - dot3(split(g), c0)
    c1 = below((l_high[1], l_low[1]), split(r1))
    c_high[PANEL:], c_low[PANEL:] = split(jnp.where((at >= TILE) | (q >= 8), c1, 0.0))


def columns_of(row_targets, column_targets, inverse, tops, firsts, pieces):
    bf16 = jnp.bfloat16
    return pl.pallas_call(
        columns_kernel,
        out_shape=[jax.ShapeDtypeStruct((2 * PANEL, 6 * TILE), bf16)] * 2
        + [jax.ShapeDtypeStruct((PANEL, PANEL), bf16)] * 2,
        in_specs=[SMEM, SMEM] + [VMEM] * 24,
        out_specs=[VMEM] * 4,
        scratch_shapes=[
            pltpu.VMEM((4, PANEL, TILE), jnp.float32),
            pltpu.VMEM((6, 2 * PANEL, TILE), jnp.float32),
        ],
        name="columns",
    )(row_targets, column_targets, *inverse, *tops, *firsts, *pieces)


def front_kernel(row_targets, column_targets, *rest):
    c_high, c_low, g_high, g_low, u_high, u_low, root = rest[:7]
    pieces = (rest[7:11], rest[11:15])
    first, others = rest[15:23], rest[23]
    factors, front, panel, child, panel_sems, child_sems = rest[24:]
    r, q = lax.axis_index("row"), lax.axis_index("col")
    x, y = q // 4, q % 4
    k = pl.program_id(0)

    def child_copies(i, source):
        return (
            pltpu.make_async_copy(first[i], child.at[source, :, :TILE], child_sems.at[source, 0]),
            pltpu.make_async_copy(others.at[source], child.at[source, :, TILE:], child_sems.at[source, 1]),
        )

    @pl.when(k == 0)
    def _():
        for part in range(2):
            for v in range(4):
                source_ref = pieces[part][v]
                for u in range(4):
                    outer, inner = NEAR[v], NEAR[u]
                    dx, dy = (inner, outer) if part == 0 else (outer, inner)
                    px, py = lax.rem(x + dx + 4, 4), lax.rem(y + dy + 4, 4)
                    half = px // 2
                    tile = jnp.where((px == 0) | (px == 3), 0, 4) + py
                    start = BLOCK * (2 * half + part)
                    pltpu.make_async_copy(
                        source_ref.at[u],
                        panel.at[tile, pl.ds(pl.multiple_of(start, BLOCK), BLOCK), :],
                        panel_sems.at[2 * half + part],
                    ).start()
        for i, (dz, dc) in enumerate(SHIFTS):
            source = shifted(r, -dz, dc)

            @pl.when(holds(row_targets, source, r))
            def _(i=i, source=source):
                for c in child_copies(i, source):
                    c.start()

    rows = PER * BLOCK
    for n in range(PER):
        arrived = panel.at[:, pl.ds(pl.multiple_of(BLOCK * (PER * k + n), BLOCK), BLOCK), :]
        pltpu.make_async_copy(arrived, arrived, panel_sems.at[PER * k + n]).wait()
    here = pl.ds(pl.multiple_of(rows * k, rows), rows)
    p0 = jnp.concatenate([panel[t, here, :] for t in range(4)], axis=1)
    p1 = jnp.concatenate([panel[t, here, :] for t in range(4, 8)], axis=1)
    at = lax.broadcasted_iota(jnp.int32, (rows, PANEL), 0)
    later = (at >= TILE) | (k > 0)
    f0 = above(split(p0), (u_high[0], u_low[0]))
    f0 = jnp.where(later | (r >= 4), f0, 0.0)
    factors[:, :PANEL] = f0
    f0 = split(f0)
    p1 = p1 - dot3(f0, (g_high[...], g_low[...]))
    f1 = above(split(p1), (u_high[1], u_low[1]))
    f1 = jnp.where(later, f1, 0.0)
    factors[:, PANEL:] = f1
    f1 = split(f1)
    both = (jnp.concatenate([f0[0], f1[0]], axis=1), jnp.concatenate([f0[1], f1[1]], axis=1))
    front[...] = root[...] - dot3(both, (c_high[...], c_low[...]))
    for c in range(2):
        for n in range(PER):
            source = 4 * c + PER * k + n

            @pl.when(holds(row_targets, source, r))
            def _(c=c, n=n, source=source):
                for copy in child_copies(0, source):
                    copy.wait()
                for m in range(3):
                    column = column_targets[c, 3 * q + m] // 16
                    columns = pl.ds(pl.multiple_of(TILE * column, TILE), TILE)
                    front[BLOCK * n : BLOCK * (n + 1), columns] += child[source, :, TILE * m : TILE * (m + 1)]


def front_of(row_targets, column_targets, columns, root, pieces, first, others):
    def whole(a):
        return pl.BlockSpec(a.shape, lambda k: (0,) * a.ndim, pipeline_mode=pl.Buffered(1))

    return pl.pallas_call(
        front_kernel,
        grid=(4 // PER,),
        out_shape=[
            jax.ShapeDtypeStruct((4 * BLOCK, 2 * PANEL), jnp.float32),
            jax.ShapeDtypeStruct((4 * BLOCK, 6 * TILE), jnp.float32),
        ],
        in_specs=[SMEM, SMEM]
        + [whole(a) for a in columns]
        + [pl.BlockSpec((PER * BLOCK, 6 * TILE), lambda k: (k, 0))]
        + [ANY] * 17,
        out_specs=[
            pl.BlockSpec((PER * BLOCK, 2 * PANEL), lambda k: (k, 0)),
            pl.BlockSpec((PER * BLOCK, 6 * TILE), lambda k: (k, 0)),
        ],
        scratch_shapes=[
            pltpu.VMEM((8, 4 * BLOCK, TILE), jnp.float32),
            pltpu.VMEM((8, BLOCK, 3 * TILE), jnp.float32),
            pltpu.SemaphoreType.DMA((4,)),
            pltpu.SemaphoreType.DMA((8, 2)),
        ],
        name="front",
    )(row_targets, column_targets, *columns, root, *pieces[0], *pieces[1], *first, others)


def near_of(x, move):
    out = [x]
    for d in NEAR[1:]:
        out.append(move(x, -d))
    return out


def along_x(v, d):
    return move_col(v, d, 0)


def along_y(v, d):
    return move_col(v, 0, d)


def steps(root_front, child_updates, row_targets, column_targets, pivot_inverse):
    r, q = lax.axis_index("row"), lax.axis_index("col")
    z, core, x = r // 2, r % 2, q // 4

    messages = pack(row_targets, child_updates, 0, TILE)
    first = [messages[0]]
    for i in range(1, 8):
        first.append(move_row(messages[i], *SHIFTS[i]))
    l_high, l_low, u_high, u_low = inverse_of(pivot_inverse)

    top = root_front[:TILE]
    tops = [top] + [None] * 7
    for i in (2, 4, 6):
        tops[i] = move_row(top, *SHIFTS[i])
    for i in (0, 2, 4, 6):
        tops[i + 1] = move_row(tops[i], 0, 1)
    upper = child_updates[2 * TILE : 4 * TILE]
    mine = jnp.where(core == 0, child_updates[: 2 * TILE], move_row(upper, 0, 1))
    moved = swap_chips(mine, (1, 0, 3, 2))
    mine = jnp.where(z % 2 == 0, mine, moved)
    theirs = swap_chips(mine, (3, 2, 1, 0))
    firsts = [mine, theirs, move_row(mine, 0, 1), move_row(theirs, 0, 1)]

    others = pack_all(row_targets, child_updates)
    others = lax.all_to_all(others, "row", 0, 0, tiled=True)

    near, far, tile = panel_of(row_targets, column_targets, root_front, first)
    far = swap_halves(far)
    piece = jnp.where(x < 2, near, far)
    a = jnp.stack(near_of(piece[:BLOCK], along_x))
    b = jnp.stack(near_of(piece[BLOCK:], along_y))
    a = near_of(a, along_y)
    b = near_of(b, along_x)

    moved = swap_chips(tile, (3, 2, 1, 0))
    tile = jnp.where(z >= 2, tile, moved)
    moved = swap_chips(tile, (1, 0, 3, 2))
    corner = jnp.stack([tile, moved])
    spread = []
    for d in (1, 2, -1):
        spread.append(move_col(corner, d, 0))
    corner = jnp.where(x == 0, corner, jnp.where(x == 1, spread[0], jnp.where(x == 2, spread[1], spread[2])))
    corners = near_of(corner, along_y)
    corners = corners + [move_row(c, 0, 1) for c in corners]
    inverse = (l_high, l_low, u_high, u_low)
    columns = columns_of(row_targets, column_targets, inverse, tops, firsts, corners)

    return front_of(
        row_targets, column_targets, [*columns, u_high, u_low], root_front, (a, b), first, others
    )


def solution(mesh):
    return jax.shard_map(
        steps,
        mesh=mesh,
        in_specs=(P("row", "col"), P("row", "col"), P(), P(), P()),
        out_specs=(P("row", None), P("row", "col")),
        check_vma=False,
    )
```

```python
import functools

import jax
import jax.numpy as jnp
from jax import lax
from jax.experimental import pallas as pl
from jax.experimental.pallas import tpu as pltpu
from jax.sharding import PartitionSpec as P

TILE = 128
PANEL = 512
BLOCK = 384
SHIFTS = ((0, 0), (0, 1), (1, 0), (1, 1), (3, 0), (3, 1), (2, 0), (2, 1))
NEAR = (0, -1, 1, 2)
ANY = pl.BlockSpec(memory_space=pl.ANY)
SMEM = pl.BlockSpec(memory_space=pltpu.SMEM)
VMEM = pl.BlockSpec(memory_space=pltpu.VMEM)
NN = (((1,), (0,)), ((), ()))


def move_row(x, dz, dc):
    pairs = [(2 * z + c, 2 * ((z + dz) % 4) + (c + dc) % 2) for z in range(4) for c in range(2)]
    return lax.ppermute(x, "row", pairs)


def swap_chips(x, other):
    return lax.ppermute(x, "row", [(2 * z + c, 2 * other[z] + c) for z in range(4) for c in range(2)])


def move_col(x, dx, dy):
    pairs = [(4 * a + b, 4 * ((a + dx) % 4) + (b + dy) % 4) for a in range(4) for b in range(4)]
    return lax.ppermute(x, "col", pairs)


def swap_halves(x):
    other = (3, 2, 1, 0)
    return lax.ppermute(x, "col", [(4 * a + b, 4 * other[a] + b) for a in range(4) for b in range(4)])


def split(x):
    high = x.astype(jnp.bfloat16)
    return high, (x - high.astype(jnp.float32)).astype(jnp.bfloat16)


def pair(x):
    return jnp.concatenate(split(x), axis=1)


def dot3(a, b):
    d = functools.partial(lax.dot_general, dimension_numbers=NN, preferred_element_type=jnp.float32)
    n, k = b.shape[1] // 2, b.shape[0] // 2
    both = d(a[0], b)
    m = n - n % PANEL
    low = d(a[1], b[:, :m])
    if n > m:
        rest = d(a[1][:, :k], b[:k, m:n]) + d(a[1][:, k:], b[k:, m:n])
        low = jnp.concatenate([low, rest], axis=1)
    return both[:, :n] + (both[:, n:] + low)


def below(l, b):
    n = PANEL // 2
    top = dot3(tuple(h[:n, :n] for h in l), b[:n])
    return jnp.concatenate([top, dot3(tuple(h[n:] for h in l), b)], axis=0)


def shifted(r, dz, dc):
    return 2 * lax.rem(r // 2 + dz + 4, 4) + lax.rem(r % 2 + dc, 2)


def child_class(targets, source, p):
    return targets[source // 4, 12 * (source % 4) + p] % 8


def holds(targets, source, r):
    hit = child_class(targets, source, 0) == r
    for p in range(1, 4):
        hit = hit | (child_class(targets, source, p) == r)
    return hit


def pack_kernel(first, last, targets, child, *outs):
    r = lax.axis_index("row")
    for i, (dz, dc) in enumerate(SHIFTS):
        dest = shifted(r, dz, dc)
        p = jnp.int32(0)
        for n in range(1, 4):
            p = jnp.where(child_class(targets, r, n) == dest, n, p)
        for j in range(3):
            rows = pl.ds(pl.multiple_of(TILE * (4 * j + p), TILE), TILE)
            outs[i][TILE * j : TILE * (j + 1), :] = child[rows, first:last]


def pack(row_targets, child, first, last):
    return pl.pallas_call(
        functools.partial(pack_kernel, first, last),
        grid=(1,),
        out_shape=[jax.ShapeDtypeStruct((BLOCK, last - first), jnp.float32)] * 8,
        in_specs=[SMEM, pl.BlockSpec((4 * BLOCK, last), lambda i: (0, 0))],
        out_specs=[VMEM] * 8,
    )(row_targets, child)


def pack_all_kernel(targets, child, out):
    r = lax.axis_index("row")
    for dest in range(8):
        p = jnp.int32(0)
        for n in range(1, 4):
            p = jnp.where(child_class(targets, r, n) == dest, n, p)
        for j in range(3):
            rows = pl.ds(pl.multiple_of(TILE * (4 * j + p), TILE), TILE)
            out[dest, TILE * j : TILE * (j + 1), :] = child[rows, TILE:]


def pack_all(row_targets, child):
    return pl.pallas_call(
        pack_all_kernel,
        grid=(1,),
        out_shape=jax.ShapeDtypeStruct((8, BLOCK, 2 * TILE), jnp.float32),
        in_specs=[SMEM, pl.BlockSpec((4 * BLOCK, 3 * TILE), lambda i: (0, 0))],
        out_specs=VMEM,
        name="pack_all",
    )(row_targets, child)


def inverse_kernel(inverse, l_high, l_low, u):
    for step in range(2):
        l_high[step], l_low[step] = split(inverse[step])
        u[step] = pair(inverse[step].T)


def inverse_of(inverse):
    return pl.pallas_call(
        inverse_kernel,
        out_shape=[jax.ShapeDtypeStruct((2, PANEL, PANEL), jnp.bfloat16)] * 2
        + [jax.ShapeDtypeStruct((2, PANEL, 2 * PANEL), jnp.bfloat16)],
        in_specs=[VMEM],
        out_specs=[VMEM] * 3,
        name="inverse",
    )(inverse)


def panel_kernel(row_targets, column_targets, root, *rest):
    messages, near, far, tile, total = rest[:8], rest[8], rest[9], rest[10], rest[11]
    r, q = lax.axis_index("row"), lax.axis_index("col")
    total[...] = root[...]
    for i, (dz, dc) in enumerate(SHIFTS):
        source = shifted(r, -dz, dc)
        first = column_targets[source // 4, 3 * q] // 16 == 0

        @pl.when(holds(row_targets, source, r) & first)
        def _(i=i, source=source):
            rows = pl.ds(pl.multiple_of(BLOCK * (source % 4), BLOCK), BLOCK)
            total[rows, :] += messages[i][...]

    near[...] = total[: 2 * BLOCK, :]
    far[...] = total[2 * BLOCK :, :]
    tile[...] = total[:TILE, :]


def panel_of(row_targets, column_targets, root, messages):
    return pl.pallas_call(
        panel_kernel,
        grid=(1,),
        out_shape=[jax.ShapeDtypeStruct((2 * BLOCK, TILE), jnp.float32)] * 2
        + [jax.ShapeDtypeStruct((TILE, TILE), jnp.float32)],
        in_specs=[SMEM, SMEM, pl.BlockSpec((4 * BLOCK, TILE), lambda i: (0, 0))] + [VMEM] * 8,
        out_specs=[VMEM] * 3,
        scratch_shapes=[pltpu.VMEM((4 * BLOCK, TILE), jnp.float32)],
        name="panel",
    )(row_targets, column_targets, root, *messages)


def first_sources(r):
    half, core = r // 4, r % 2
    return (half, core), (1 - half, core), (half, 1 - core), (1 - half, 1 - core)


def columns_kernel(row_targets, column_targets, l_high, l_low, u, *rest):
    tops, firsts, pieces = rest[:8], rest[8:12], rest[12:20]
    c, g_out, corner, rows = rest[20:]
    r, q = lax.axis_index("row"), lax.axis_index("col")
    for piece, (dz, dc) in zip(tops, SHIFTS, strict=True):
        here = pl.ds(pl.multiple_of(TILE * shifted(r, -dz, dc), TILE), TILE)
        for m in range(6):
            rows[m, here, :] = piece[:, TILE * m : TILE * (m + 1)]
    for piece, (child, part) in zip(firsts, first_sources(r), strict=True):
        for n in range(2):
            here = pl.ds(pl.multiple_of(TILE * row_targets[child, 2 * part + n], TILE), TILE)
            for m in range(3):
                column = column_targets[child, 3 * q + m] // 16
                rows[column, here, :] += piece[TILE * n : TILE * (n + 1), TILE * m : TILE * (m + 1)]
    core = r % 2
    for n, piece in enumerate(pieces):
        part = core if n < 4 else 1 - core
        tile = lax.rem(q % 4 + NEAR[n % 4] + 4, 4)
        chip = jnp.where(r // 2 >= 2, r // 2, 3 - r // 2)
        for m in range(2):
            below_first = 2 * (chip if m == 0 else 5 - chip) + part - 4
            corner[tile, pl.ds(pl.multiple_of(TILE * below_first, TILE), TILE), :] = piece[m]
    block = jnp.concatenate([corner[t] for t in range(4)], axis=1)
    g = dot3(split(block), u[0])
    g_out[...] = pair(g.T)
    at = lax.broadcasted_iota(jnp.int32, (PANEL, 6 * TILE), 1)
    r0 = jnp.concatenate([rows[m, :PANEL] for m in range(6)], axis=1)
    c0 = below((l_high[0], l_low[0]), pair(r0))
    c0 = pair(jnp.where((at >= TILE) | (q >= 4), c0, 0.0))
    c[:PANEL] = c0
    r1 = jnp.concatenate([rows[m, PANEL:] for m in range(6)], axis=1)
    r1 = r1 - dot3(split(g), c0)
    c1 = below((l_high[1], l_low[1]), pair(r1))
    c[PANEL:] = pair(jnp.where((at >= TILE) | (q >= 8), c1, 0.0))


def columns_of(row_targets, column_targets, inverse, tops, firsts, pieces):
    bf16 = jnp.bfloat16
    return pl.pallas_call(
        columns_kernel,
        out_shape=[
            jax.ShapeDtypeStruct((2 * PANEL, 12 * TILE), bf16),
            jax.ShapeDtypeStruct((PANEL, 2 * PANEL), bf16),
        ],
        in_specs=[SMEM, SMEM] + [VMEM] * 23,
        out_specs=[VMEM] * 2,
        scratch_shapes=[
            pltpu.VMEM((4, PANEL, TILE), jnp.float32),
            pltpu.VMEM((6, 2 * PANEL, TILE), jnp.float32),
        ],
        name="columns",
    )(row_targets, column_targets, *inverse, *tops, *firsts, *pieces)


def front_kernel(part, row_targets, column_targets, *rest):
    sources, root = rest[:3], rest[3]
    pieces, first, others = rest[4:8], rest[8:16], rest[16]
    factors, front, panel, child, c, g, u, panel_sems, child_sems, sems = rest[-10:]
    r, q = lax.axis_index("row"), lax.axis_index("col")
    x, y = q // 4, q % 4
    k = pl.program_id(0)
    block = 2 * k + part

    def child_copies(i, source):
        return (
            pltpu.make_async_copy(first[i], child.at[source, :, :TILE], child_sems.at[source, 0]),
            pltpu.make_async_copy(others.at[source], child.at[source, :, TILE:], child_sems.at[source, 1]),
        )

    held = [
        pltpu.make_async_copy(source, here, sems.at[i])
        for i, (source, here) in enumerate(zip(sources, (c, g, u), strict=True))
    ]

    @pl.when(k == 0)
    def _():
        held[2].start()
        for v in range(4):
            for w in range(4):
                outer, inner = NEAR[v], NEAR[w]
                dx, dy = (inner, outer) if part == 0 else (outer, inner)
                px, py = lax.rem(x + dx + 4, 4), lax.rem(y + dy + 4, 4)
                tile = jnp.where((px == 0) | (px == 3), 0, 4) + py
                pltpu.make_async_copy(
                    pieces[v].at[w], panel.at[px // 2, tile], panel_sems.at[px // 2]
                ).start()
        held[1].start()
        held[0].start()
        for i, (dz, dc) in enumerate(SHIFTS):
            source = shifted(r, -dz, dc)

            @pl.when(holds(row_targets, source, r) & (source % 2 == part))
            def _(i=i, source=source):
                for copy in child_copies(i, source):
                    copy.start()

    @pl.when(k == 0)
    def _():
        held[2].wait()
        held[1].wait()

    pltpu.make_async_copy(panel.at[k], panel.at[k], panel_sems.at[k]).wait()
    p0 = jnp.concatenate([panel[k, t] for t in range(4)], axis=1)
    p1 = jnp.concatenate([panel[k, t] for t in range(4, 8)], axis=1)
    at = lax.broadcasted_iota(jnp.int32, (BLOCK, PANEL), 0)
    later = (at >= TILE) | (block > 0)
    f0 = dot3(split(p0), u[0])
    f0 = jnp.where(later | (r >= 4), f0, 0.0)
    factors[:, :PANEL] = f0
    f0 = split(f0)
    p1 = p1 - dot3(f0, g[...])
    f1 = dot3(split(p1), u[1])
    f1 = jnp.where(later, f1, 0.0)
    factors[:, PANEL:] = f1
    f1 = split(f1)

    @pl.when(k == 0)
    def _():
        held[0].wait()

    both = (jnp.concatenate([f0[0], f1[0]], axis=1), jnp.concatenate([f0[1], f1[1]], axis=1))
    front[...] = root[...] - dot3(both, c[...])
    for half in range(2):
        source = 4 * half + block

        @pl.when(holds(row_targets, source, r))
        def _(half=half, source=source):
            for copy in child_copies(0, source):
                copy.wait()
            for m in range(3):
                column = column_targets[half, 3 * q + m] // 16
                columns = pl.ds(pl.multiple_of(TILE * column, TILE), TILE)
                front[:, columns] += child[source, :, TILE * m : TILE * (m + 1)]


def front_of(part, row_targets, column_targets, columns, root, pieces, first, others, done=()):
    return pl.pallas_call(
        functools.partial(front_kernel, part),
        grid=(2,),
        out_shape=[
            jax.ShapeDtypeStruct((4 * BLOCK, 2 * PANEL), jnp.float32),
            jax.ShapeDtypeStruct((4 * BLOCK, 6 * TILE), jnp.float32),
        ],
        in_specs=[SMEM, SMEM]
        + [ANY] * 3
        + [pl.BlockSpec((BLOCK, 6 * TILE), lambda k: (2 * k + part, 0))]
        + [ANY] * (13 + len(done)),
        out_specs=[
            pl.BlockSpec((BLOCK, 2 * PANEL), lambda k: (2 * k + part, 0)),
            pl.BlockSpec((BLOCK, 6 * TILE), lambda k: (2 * k + part, 0)),
        ],
        scratch_shapes=[
            pltpu.VMEM((2, 8, BLOCK, TILE), jnp.float32),
            pltpu.VMEM((8, BLOCK, 3 * TILE), jnp.float32),
            *(pltpu.VMEM(a.shape, a.dtype) for a in columns),
            pltpu.SemaphoreType.DMA((2,)),
            pltpu.SemaphoreType.DMA((8, 2)),
            pltpu.SemaphoreType.DMA((3,)),
        ],
        input_output_aliases={19: 0, 20: 1} if done else {},
    )(row_targets, column_targets, *columns, root, *pieces, *first, others, *done)


def near_of(x, move):
    out = [x]
    for d in NEAR[1:]:
        out.append(move(x, -d))
    return out


def along_x(v, d):
    return move_col(v, d, 0)


def along_y(v, d):
    return move_col(v, 0, d)


def steps(root_front, child_updates, row_targets, column_targets, pivot_inverse):
    r, q = lax.axis_index("row"), lax.axis_index("col")
    z, core, x = r // 2, r % 2, q // 4

    messages = pack(row_targets, child_updates, 0, TILE)
    first = [messages[0]]
    for i in range(1, 8):
        first.append(move_row(messages[i], *SHIFTS[i]))
    l_high, l_low, u = inverse_of(pivot_inverse)

    top = root_front[:TILE]
    tops = [top] + [None] * 7
    for i in (2, 4, 6):
        tops[i] = move_row(top, *SHIFTS[i])
    for i in (0, 2, 4, 6):
        tops[i + 1] = move_row(tops[i], 0, 1)
    upper = child_updates[2 * TILE : 4 * TILE]
    mine = jnp.where(core == 0, child_updates[: 2 * TILE], move_row(upper, 0, 1))
    moved = swap_chips(mine, (1, 0, 3, 2))
    mine = jnp.where(z % 2 == 0, mine, moved)
    theirs = swap_chips(mine, (3, 2, 1, 0))
    firsts = [mine, theirs, move_row(mine, 0, 1), move_row(theirs, 0, 1)]

    others = pack_all(row_targets, child_updates)
    others = lax.all_to_all(others, "row", 0, 0, tiled=True)

    near, far, tile = panel_of(row_targets, column_targets, root_front, first)
    far = swap_halves(far)
    piece = jnp.where(x < 2, near, far)
    a = jnp.stack(near_of(piece[:BLOCK], along_x))
    b = jnp.stack(near_of(piece[BLOCK:], along_y))
    a = near_of(a, along_y)
    b = near_of(b, along_x)

    moved = swap_chips(tile, (3, 2, 1, 0))
    tile = jnp.where(z >= 2, tile, moved)
    moved = swap_chips(tile, (1, 0, 3, 2))
    corner = jnp.stack([tile, moved])
    spread = []
    for d in (1, 2, -1):
        spread.append(move_col(corner, d, 0))
    corner = jnp.where(x == 0, corner, jnp.where(x == 1, spread[0], jnp.where(x == 2, spread[1], spread[2])))
    corners = near_of(corner, along_y)
    corners = corners + [move_row(c, 0, 1) for c in corners]
    inverse = (l_high, l_low, u)
    columns = columns_of(row_targets, column_targets, inverse, tops, firsts, corners)

    front = functools.partial(front_of, row_targets=row_targets, column_targets=column_targets)
    front = functools.partial(front, columns=[*columns, u], root=root_front, first=first, others=others)
    done = front(1, pieces=b)
    return front(0, pieces=a, done=done)


def solution(mesh):
    return jax.shard_map(
        steps,
        mesh=mesh,
        in_specs=(P("row", "col"), P("row", "col"), P(), P(), P()),
        out_specs=(P("row", None), P("row", "col")),
        check_vma=False,
    )
```
